32 devices in a mesh: group: 2 (over y), section: 4 (over z), span: 2 (over x), mp: 2 (over core).
Axes of the slice: x: 2, y: 2, z: 4, core: 2. Of those that a mesh axis runs over, the one named last changes fastest.
Arguments:
- queries: bfloat16 [8, 256, 4096], P(('group', 'section'), None, ('span', 'mp')), parts along dimension 0, may hold values from -5 to 5
- keys_values: bfloat16 [2, 8, 256, 4096], P(None, ('group', 'section'), None, ('span', 'mp')), parts along dimension 1, may hold values from -5 to 5
- latents: bfloat16 [8, 256, 5120], P(('group', 'section'), ('span', 'mp')), parts along dimension 0, may hold values from -6 to 6
- out_weight: bfloat16 [4096, 5120], P(('span', 'mp')), may hold values from -3 to 3
- gate_table: float32 [8, 5120], replicated, may hold values from 0.5 to 1.5
- level_index: int32 [8], P(('group', 'section')), parts along dimension 0, may hold values from 0 to 7
- pair_window: int32 [6], P('group'), parts along dimension 0, may hold values from 0 to 256
Outputs:
- shifted: bfloat16 [8, 256, 5120], P(('group', 'section'), ('span', 'mp')), parts along dimension 0
The draws below stay inside these ranges and needn't reach their ends.
There are 2 independent parts, one for each index of `group`. The reference program is written for one: setup_inputs(seed, part) draws one part's arguments, and reference() takes and returns one part's arrays. A program takes and returns all parts, laid end to end along the dimension named above; an argument that names none is the same for every part. Nothing has to cross between parts.
All inputs are finite; a program needn't handle non-finite values.
Results may differ from the reference program's by a relative error of at most 0.015.
Values may be sent and summed in bfloat16 or wider, within the bound.
A program may use at most 64 MiB of HBM per device.

```python
import math
import jax
import jax.numpy as jnp
from jax import lax

D = 5120
HD = 128
LEVELS = 8
SPAN_TOK = 256
NS = 4
HQ = 4096


def draw_triple(key):
    key_query, key_keys, key_values = jax.random.split(jax.random.fold_in(key, 7), 3)
    full_shape = (NS, SPAN_TOK, HQ)
    query_draw = jnp.clip(jax.random.normal(key_query, full_shape, jnp.float32), -5.0, 5.0)
    keys_draw = jnp.clip(jax.random.normal(key_keys, full_shape, jnp.float32), -5.0, 5.0)
    values_draw = jnp.clip(jax.random.normal(key_values, full_shape, jnp.float32), -5.0, 5.0)
    return (query_draw, keys_draw, values_draw)


def draw_queries(key, part):
    return draw_triple(key)[0].astype(jnp.bfloat16)


def draw_keys_values(key, part):
    triple = draw_triple(key)
    return jnp.stack([triple[1], triple[2]], 0).astype(jnp.bfloat16)


def draw_pair_window(key, part):
    key_rows, key_spot = jax.random.split(jax.random.fold_in(key, 11), 2)
    pair_count = NS - 1
    widths = jax.random.randint(key_rows, (pair_count,), 0, SPAN_TOK + 1)
    spot = jax.random.randint(key_spot, (), 0, pair_count)
    other = (spot + 1) % pair_count
    places = jnp.arange(pair_count, dtype=jnp.int32)
    widths = jnp.where(places == spot, SPAN_TOK, widths)
    widths = jnp.where(places == other, 0, widths)
    return widths.astype(jnp.int32)


def with_ends(values, rng, smallest, top_value):
    dims = values.shape
    index_at = [jax.random.randint(jax.random.fold_in(rng, axis), (), 0, dims[axis]) for axis in range(len(dims))]
    values = values.at[tuple(index_at)].set(smallest)
    longest = dims.index(max(dims))
    index_at[longest] = (index_at[longest] + 1) % dims[longest]
    return values.at[tuple(index_at)].set(top_value)


def block_scale(own_key, dims, pieces, least, top_value):
    factor_of, own = 1.0, jax.random.fold_in(own_key, 6)
    for position, parts in pieces:
        draws = jnp.exp(jax.random.uniform(jax.random.fold_in(own, position), (parts,), jnp.float32, least / len(pieces), top_value / len(pieces)))
        factor_of = factor_of * jnp.repeat(draws, dims[position] // parts).reshape([-1 if axis == position else 1 for axis in range(len(dims))])
    return factor_of


def gaussian(key, shape, scale, most, cuts=(), kind=jnp.bfloat16):
    loudness = block_scale(key, shape, cuts, -0.22, 0.18) if cuts else 1.0
    entries = jax.random.normal(key, shape, jnp.float32) * scale * loudness
    return jnp.minimum(jnp.maximum(entries, -most), most).astype(kind)


def setup_inputs(seed: int = 0, part: int = 0) -> dict:
    key_of = jax.random.split(jax.random.key(seed), 8)
    part_splits = jax.random.split(jax.random.fold_in(key_of[7], part), 8)
    return {
        "queries": draw_queries(jax.random.fold_in(jax.random.fold_in(key_of[7], part), 71), part),
        "keys_values": draw_keys_values(jax.random.fold_in(jax.random.fold_in(key_of[7], part), 71), part),
        "latents": gaussian(part_splits[2], (NS, SPAN_TOK, D), 1.0, 6.0, ((0, 4), (1, 4))),
        "out_weight": gaussian(key_of[3], (HQ, D), (max(HD // 32, 1)) ** -0.5, 3.0, ((0, 4),)),
        "gate_table": jnp.clip(jax.random.uniform(key_of[4], (LEVELS, D), jnp.float32, 0.5, 1.5), 0.5, 1.5),
        "level_index": with_ends(jax.random.randint(part_splits[5], (NS,), 0, LEVELS), jax.random.fold_in(part_splits[5], 1), 0, LEVELS - 1).astype(jnp.int32),
        "pair_window": draw_pair_window(jax.random.fold_in(jax.random.fold_in(key_of[7], part), 71), part),
    }


NEG_BIG = -1e+30

def reference(queries, keys_values, latents, out_weight, gate_table, level_index, pair_window):
    sections, span_tok, width_all = queries.shape
    head_count = width_all // HD
    score_scale = 1.0 / math.sqrt(HD)
    final_pair = sections - 2
    row_ids = jnp.arange(span_tok, dtype=jnp.int32)

    def one_section(section_id):
        prev_width = jnp.where(section_id > 0, pair_window[jnp.clip(section_id - 1, 0, final_pair)], 0)
        next_width = jnp.where(section_id < sections - 1, pair_window[jnp.clip(section_id, 0, final_pair)], 0)
        lower_id = jnp.clip(section_id - 1, 0, sections - 1)
        upper_id = jnp.clip(section_id + 1, 0, sections - 1)
        key_rows = jnp.concatenate([keys_values[0, lower_id], keys_values[0, section_id], keys_values[0, upper_id]], 0)
        value_rows = jnp.concatenate([keys_values[1, lower_id], keys_values[1, section_id], keys_values[1, upper_id]], 0)
        key_mask = jnp.concatenate([row_ids >= span_tok - prev_width, jnp.ones((span_tok,), bool), row_ids < next_width], 0)
        query_rows = queries[section_id]

        def one_head(head_id):
            col_start = head_id * HD
            query_head = lax.dynamic_slice_in_dim(query_rows, col_start, HD, 1)
            key_head = lax.dynamic_slice_in_dim(key_rows, col_start, HD, 1)
            value_head = lax.dynamic_slice_in_dim(value_rows, col_start, HD, 1)
            scores = jnp.dot(query_head, key_head.T, preferred_element_type=jnp.float32) * score_scale
            scores = jnp.where(key_mask[None, :], scores, NEG_BIG)
            row_max = lax.optimization_barrier(jnp.max(scores, axis=1, keepdims=True))
            probabilities = jnp.where(key_mask[None, :], jnp.exp(scores - row_max), 0.0)
            row_total = lax.optimization_barrier(jnp.sum(probabilities, axis=1, keepdims=True))
            weighted = jnp.dot(probabilities.astype(jnp.bfloat16), value_head, preferred_element_type=jnp.float32)
            return (weighted / row_total).astype(jnp.bfloat16)
        per_head = lax.map(one_head, jnp.arange(head_count, dtype=jnp.int32))
        attended = jnp.transpose(per_head, (1, 0, 2)).reshape(span_tok, width_all)
        projected = jnp.dot(attended, out_weight, preferred_element_type=jnp.float32)
        gate_row = gate_table[level_index[section_id]]
        return (latents[section_id].astype(jnp.float32) + gate_row[None, :] * projected).astype(jnp.bfloat16)
    updated = lax.map(one_section, jnp.arange(sections, dtype=jnp.int32))
    return jnp.roll(updated, 1, axis=0)
```

```python
import functools
import math

import jax
import jax.numpy as jnp
from jax import lax
from jax.experimental import pallas as pl
from jax.experimental.pallas import tpu as pltpu
from jax.sharding import PartitionSpec as P

HD = 128
NEG_BIG = -1e30
CHUNK = 256
LAG_MP = 4
LAG_SPAN = 10


def fused(
    sections, spans, mps, chunk, lag_mp, lag_span,
    level_ref, window_ref, q_hbm, kv_hbm, lat_hbm, w_hbm, gate_hbm, out_hbm,
    q_buf, kv_buf, lat_buf, w_buf, gate_buf, below, above, att, keep,
    send_mp, recv_mp, send_span, recv_span, send_next,
    load_sems, up_send, up_recv, down_send, down_recv,
    mp_send, mp_recv, span_send, span_recv, next_send, next_recv, relay,
):
    s = lax.axis_index("section")
    x = lax.axis_index("span")
    m = lax.axis_index("mp")
    last = sections - 1
    heads = below.shape[0]
    tokens = kv_buf.shape[1]
    width = kv_buf.shape[2]
    rows = lat_buf.shape[0]
    chunks = keep.shape[0]
    succ = lax.rem(s + 1, sections)
    pred = lax.rem(s + sections - 1, sections)

    barrier = pltpu.get_barrier_semaphore()

    @pl.when(s < last)
    def _():
        pl.semaphore_signal(barrier, 1, device_id={"section": succ})

    @pl.when(s > 0)
    def _():
        pl.semaphore_signal(barrier, 1, device_id={"section": pred})

    for j in range(1, mps):
        pl.semaphore_signal(barrier, 1, device_id={"mp": lax.rem(m + j, mps)})
    for i in range(1, spans):
        pl.semaphore_signal(barrier, 1, device_id={"span": lax.rem(x + i, spans)})
    others = mps - 1 + spans - 1

    loads = [
        pltpu.make_async_copy(q_hbm.at[0], q_buf, load_sems.at[0]),
        pltpu.make_async_copy(kv_hbm.at[:, 0], kv_buf, load_sems.at[1]),
        pltpu.make_async_copy(lat_hbm.at[0], lat_buf, load_sems.at[2]),
        pltpu.make_async_copy(gate_hbm, gate_buf, load_sems.at[3]),
        pltpu.make_async_copy(w_hbm, w_buf, load_sems.at[4]),
    ]

    @pl.when((s > 0) & (s < last))
    def _():
        pl.semaphore_wait(barrier, others + 2)

    @pl.when((s == 0) | (s == last))
    def _():
        pl.semaphore_wait(barrier, others + 1)

    def head_cols(h):
        return pl.ds(pl.multiple_of(h * HD, HD), HD)

    def chunk_cols(c):
        return pl.ds(pl.multiple_of(c * chunk, chunk), chunk)

    def up(h):
        return pltpu.make_async_remote_copy(
            kv_hbm.at[:, 0, :, head_cols(h)], below.at[h], up_send.at[h], up_recv.at[h],
            device_id={"section": succ},
        )

    def down(h):
        return pltpu.make_async_remote_copy(
            kv_hbm.at[:, 0, :, head_cols(h)], above.at[h], down_send.at[h], down_recv.at[h],
            device_id={"section": pred},
        )

    @pl.loop(0, heads)
    def _(h):
        @pl.when(s < last)
        def _():
            up(h).start()

        @pl.when(s > 0)
        def _():
            down(h).start()

    for load in loads:
        load.start()

    @pl.when(s == 0)
    def _():
        below[...] = jnp.zeros_like(below)
        pl.semaphore_signal(relay, 1, device_id={"section": succ})

    @pl.when(s == last)
    def _():
        above[...] = jnp.zeros_like(above)

    pairs = window_ref.shape[0]
    w_lo = jnp.where(s > 0, window_ref[jnp.clip(s - 1, 0, pairs - 1)], 0)
    w_hi = jnp.where(s < last, window_ref[jnp.clip(s, 0, pairs - 1)], 0)
    key_ids = lax.broadcasted_iota(jnp.int32, (1, tokens), 1)
    mask_lo = key_ids >= tokens - w_lo
    mask_hi = key_ids < w_hi
    scale = 1.0 / math.sqrt(HD)
    loads[0].wait()
    loads[1].wait()

    def score(q, k):
        return lax.dot_general(
            q, k, (((1,), (1,)), ((), ())), preferred_element_type=jnp.float32
        ) * scale

    @pl.loop(0, heads)
    def _(h):
        cols = head_cols(h)

        @pl.when(s > 0)
        def _():
            up(h).wait_recv()

        @pl.when(s < last)
        def _():
            down(h).wait_recv()

        q = q_buf[:, cols]
        s_own = score(q, kv_buf[0, :, cols])
        s_lo = jnp.where(mask_lo, score(q, below[h, 0]), NEG_BIG)
        s_hi = jnp.where(mask_hi, score(q, above[h, 0]), NEG_BIG)
        top = jnp.max(jnp.maximum(jnp.maximum(s_lo, s_hi), s_own), axis=1, keepdims=True)
        p_lo = jnp.exp(s_lo - top)
        p_own = jnp.exp(s_own - top)
        p_hi = jnp.exp(s_hi - top)
        total = jnp.sum(p_lo + p_own + p_hi, axis=1, keepdims=True)
        weighted = (
            jnp.dot(p_own.astype(jnp.bfloat16), kv_buf[1, :, cols], preferred_element_type=jnp.float32)
            + jnp.dot(p_lo.astype(jnp.bfloat16), below[h, 1], preferred_element_type=jnp.float32)
            + jnp.dot(p_hi.astype(jnp.bfloat16), above[h, 1], preferred_element_type=jnp.float32)
        )
        result = (weighted / total).astype(jnp.bfloat16).reshape(spans, mps, rows, HD)
        for xb in range(spans):
            for mb in range(mps):
                att[lax.rem(mb - m + mps, mps), lax.rem(xb - x + spans, spans), :, cols] = result[xb, mb]

    @pl.when((s > 0) & (s < last))
    def _():
        pl.semaphore_wait(relay, 1)
        pl.semaphore_signal(relay, 1, device_id={"section": succ})

    @pl.when(s == last)
    def _():
        pl.semaphore_wait(relay, 1)

    for load in loads[2:]:
        load.wait()
    level = level_ref[0]

    def to_mp(j, c):
        return pltpu.make_async_remote_copy(
            send_mp.at[j - 1, c], recv_mp.at[j - 1, c], mp_send.at[j - 1, c], mp_recv.at[j - 1, c],
            device_id={"mp": lax.rem(m + j, mps)},
        )

    def to_span(i, c):
        return pltpu.make_async_remote_copy(
            send_span.at[i - 1, c], recv_span.at[i - 1, c],
            span_send.at[i - 1, c], span_recv.at[i - 1, c],
            device_id={"span": lax.rem(x + i, spans)},
        )

    def to_next(c):
        return pltpu.make_async_remote_copy(
            send_next.at[c], out_hbm.at[0, :, chunk_cols(c)], next_send.at[c], next_recv.at[c],
            device_id={"section": succ},
        )

    def project(c):
        part = jnp.dot(
            att[...].reshape(tokens, width), w_buf[:, chunk_cols(c)],
            preferred_element_type=jnp.float32,
        ).reshape(mps, spans, rows, chunk)
        for j in range(1, mps):
            send_mp[j - 1, c] = part[j].astype(jnp.bfloat16)
            to_mp(j, c).start()
        keep[c] = part[0]

    def reduce_mp(c):
        total = keep[c]
        for j in range(1, mps):
            to_mp(j, c).wait_recv()
            total = total + recv_mp[j - 1, c].astype(jnp.float32)
        for i in range(1, spans):
            send_span[i - 1, c] = total[i].astype(jnp.bfloat16)
            to_span(i, c).start()
        keep[c, 0] = total[0]

    def finish(c):
        total = keep[c, 0]
        for i in range(1, spans):
            to_span(i, c).wait_recv()
            total = total + recv_span[i - 1, c].astype(jnp.float32)
        table = gate_buf[:, chunk_cols(c)]
        level_ids = lax.broadcasted_iota(jnp.int32, table.shape, 0)
        gate = jnp.sum(jnp.where(level_ids == level, table, 0.0), axis=0, keepdims=True)
        updated = lat_buf[:, chunk_cols(c)].astype(jnp.float32) + gate * total
        send_next[c] = updated.astype(jnp.bfloat16)
        to_next(c).start()

    @pl.loop(0, chunks + lag_span)
    def _(step):
        @pl.when(step < chunks)
        def _():
            project(step)

        @pl.when((step >= lag_mp) & (step < chunks + lag_mp))
        def _():
            reduce_mp(step - lag_mp)

        @pl.when(step >= lag_span)
        def _():
            finish(step - lag_span)

    @pl.loop(0, heads)
    def _(h):
        @pl.when(s < last)
        def _():
            up(h).wait_send()

        @pl.when(s > 0)
        def _():
            down(h).wait_send()

    @pl.loop(0, chunks)
    def _(c):
        for j in range(1, mps):
            to_mp(j, c).wait_send()
        for i in range(1, spans):
            to_span(i, c).wait_send()
        to_next(c).wait()


def shards(sizes, queries, keys_values, latents, out_weight, gate_table, level_index, pair_window):
    sections, spans, mps = sizes
    tokens, width = queries.shape[1:]
    rows, model = latents.shape[1:]
    heads = width // HD
    chunk = CHUNK if model % CHUNK == 0 else HD
    chunks = model // chunk
    bf16, f32 = jnp.bfloat16, jnp.float32
    dma = pltpu.SemaphoreType.DMA
    hbm = pl.BlockSpec(memory_space=pltpu.HBM)
    smem = pl.BlockSpec(memory_space=pltpu.SMEM)
    return pl.pallas_call(
        functools.partial(fused, sections, spans, mps, chunk, LAG_MP, LAG_SPAN),
        out_shape=jax.ShapeDtypeStruct(latents.shape, bf16),
        in_specs=[smem, smem, hbm, hbm, hbm, hbm, hbm],
        out_specs=hbm,
        scratch_shapes=[
            pltpu.VMEM((tokens, width), bf16),
            pltpu.VMEM((2, tokens, width), bf16),
            pltpu.VMEM((rows, model), bf16),
            pltpu.VMEM(out_weight.shape, bf16),
            pltpu.VMEM(gate_table.shape, f32),
            pltpu.VMEM((heads, 2, tokens, HD), bf16),
            pltpu.VMEM((heads, 2, tokens, HD), bf16),
            pltpu.VMEM((mps, spans, rows, width), bf16),
            pltpu.VMEM((chunks, spans, rows, chunk), f32),
            pltpu.VMEM((mps - 1, chunks, spans, rows, chunk), bf16),
            pltpu.VMEM((mps - 1, chunks, spans, rows, chunk), bf16),
            pltpu.VMEM((spans - 1, chunks, rows, chunk), bf16),
            pltpu.VMEM((spans - 1, chunks, rows, chunk), bf16),
            pltpu.VMEM((chunks, rows, chunk), bf16),
            dma((5,)),
            dma((heads,)), dma((heads,)), dma((heads,)), dma((heads,)),
            dma((mps - 1, chunks)), dma((mps - 1, chunks)),
            dma((spans - 1, chunks)), dma((spans - 1, chunks)),
            dma((chunks,)), dma((chunks,)),
            pltpu.SemaphoreType.REGULAR,
        ],
        compiler_params=pltpu.CompilerParams(
            collective_id=0, has_side_effects=True, vmem_limit_bytes=60 * 1024 * 1024
        ),
    )(level_index, pair_window, queries, keys_values, latents, out_weight, gate_table)


def solution(mesh):
    sizes = (mesh.shape["section"], mesh.shape["span"], mesh.shape["mp"])
    in_specs = (
        P(("group", "section"), None, ("span", "mp")),
        P(None, ("group", "section"), None, ("span", "mp")),
        P(("group", "section"), ("span", "mp"), None),
        P(("span", "mp"), None),
        P(),
        P(("group", "section")),
        P("group"),
    )
    out_specs = P(("group", "section"), ("span", "mp"), None)
    return jax.shard_map(
        functools.partial(shards, sizes), mesh=mesh, in_specs=in_specs, out_specs=out_specs,
        check_vma=False,
    )
```

```python
import functools
import math

import jax
import jax.numpy as jnp
from jax import lax
from jax.experimental import pallas as pl
from jax.experimental.pallas import tpu as pltpu
from jax.sharding import PartitionSpec as P

HD = 128
NEG_BIG = -1e30
CHUNK = 256
LAG_MP = 3
LAG_SPAN = 8


def fused(
    sections, spans, mps, chunk, lag_mp, lag_span,
    level_hbm, window_hbm, q_hbm, kv_hbm, lat_hbm, w_hbm, gate_hbm, out_hbm,
    q_buf, kv_buf, lat_buf, w_buf, gate_buf, below, above, att, keep,
    send_mp, recv_mp, send_span, recv_span, send_next,
    level_ref, window_ref, load_sems, up_send, up_recv, down_send, down_recv,
    mp_send, mp_recv, span_send, span_recv, next_send, next_recv, relay,
):
    s = lax.axis_index("section")
    x = lax.axis_index("span")
    m = lax.axis_index("mp")
    last = sections - 1
    heads = below.shape[0]
    tokens = kv_buf.shape[1]
    width = kv_buf.shape[2]
    rows = lat_buf.shape[0]
    chunks = keep.shape[0]
    succ = lax.rem(s + 1, sections)
    pred = lax.rem(s + sections - 1, sections)

    barrier = pltpu.get_barrier_semaphore()

    @pl.when(s < last)
    def _():
        pl.semaphore_signal(barrier, 1, device_id={"section": succ})

    @pl.when(s > 0)
    def _():
        pl.semaphore_signal(barrier, 1, device_id={"section": pred})

    for j in range(1, mps):
        pl.semaphore_signal(barrier, 1, device_id={"mp": lax.rem(m + j, mps)})
    for i in range(1, spans):
        pl.semaphore_signal(barrier, 1, device_id={"span": lax.rem(x + i, spans)})
    others = mps - 1 + spans - 1

    windows = pltpu.make_async_copy(window_hbm, window_ref, load_sems.at[6])
    loads = [
        pltpu.make_async_copy(q_hbm.at[0], q_buf, load_sems.at[0]),
        pltpu.make_async_copy(kv_hbm.at[:, 0], kv_buf, load_sems.at[1]),
        pltpu.make_async_copy(lat_hbm.at[0], lat_buf, load_sems.at[2]),
        pltpu.make_async_copy(gate_hbm, gate_buf, load_sems.at[3]),
        pltpu.make_async_copy(w_hbm, w_buf, load_sems.at[4]),
        pltpu.make_async_copy(level_hbm, level_ref, load_sems.at[5]),
    ]

    @pl.when((s > 0) & (s < last))
    def _():
        pl.semaphore_wait(barrier, others + 2)

    @pl.when((s == 0) | (s == last))
    def _():
        pl.semaphore_wait(barrier, others + 1)

    def head_cols(h):
        return pl.ds(pl.multiple_of(h * HD, HD), HD)

    def chunk_cols(c):
        return pl.ds(pl.multiple_of(c * chunk, chunk), chunk)

    def up(h):
        return pltpu.make_async_remote_copy(
            kv_hbm.at[:, 0, :, head_cols(h)], below.at[h], up_send.at[h], up_recv.at[h],
            device_id={"section": succ},
        )

    def down(h):
        return pltpu.make_async_remote_copy(
            kv_hbm.at[:, 0, :, head_cols(h)], above.at[h], down_send.at[h], down_recv.at[h],
            device_id={"section": pred},
        )

    @pl.loop(0, heads)
    def _(h):
        @pl.when(s < last)
        def _():
            up(h).start()

        @pl.when(s > 0)
        def _():
            down(h).start()

    windows.start()
    for load in loads:
        load.start()

    @pl.when(s == 0)
    def _():
        below[...] = jnp.zeros_like(below)
        pl.semaphore_signal(relay, 1, device_id={"section": succ})

    @pl.when(s == last)
    def _():
        above[...] = jnp.zeros_like(above)

    windows.wait()
    pairs = window_ref.shape[0]
    w_lo = jnp.where(s > 0, window_ref[jnp.clip(s - 1, 0, pairs - 1)], 0)
    w_hi = jnp.where(s < last, window_ref[jnp.clip(s, 0, pairs - 1)], 0)
    key_ids = lax.broadcasted_iota(jnp.int32, (1, tokens), 1)
    mask_lo = key_ids >= tokens - w_lo
    mask_hi = key_ids < w_hi
    scale = 1.0 / math.sqrt(HD)
    loads[0].wait()
    loads[1].wait()

    def score(q, k):
        return lax.dot_general(
            q, k, (((1,), (1,)), ((), ())), preferred_element_type=jnp.float32
        ) * scale

    @pl.loop(0, heads)
    def _(h):
        cols = head_cols(h)

        @pl.when(s > 0)
        def _():
            up(h).wait_recv()

        @pl.when(s < last)
        def _():
            down(h).wait_recv()

        q = q_buf[:, cols]
        s_own = score(q, kv_buf[0, :, cols])
        s_lo = jnp.where(mask_lo, score(q, below[h, 0]), NEG_BIG)
        s_hi = jnp.where(mask_hi, score(q, above[h, 0]), NEG_BIG)
        top = jnp.max(jnp.maximum(jnp.maximum(s_lo, s_hi), s_own), axis=1, keepdims=True)
        p_lo = jnp.exp(s_lo - top)
        p_own = jnp.exp(s_own - top)
        p_hi = jnp.exp(s_hi - top)
        total = jnp.sum(p_lo + p_own + p_hi, axis=1, keepdims=True)
        weighted = (
            jnp.dot(p_own.astype(jnp.bfloat16), kv_buf[1, :, cols], preferred_element_type=jnp.float32)
            + jnp.dot(p_lo.astype(jnp.bfloat16), below[h, 1], preferred_element_type=jnp.float32)
            + jnp.dot(p_hi.astype(jnp.bfloat16), above[h, 1], preferred_element_type=jnp.float32)
        )
        result = (weighted / total).astype(jnp.bfloat16).reshape(spans, mps, rows, HD)
        for xb in range(spans):
            for mb in range(mps):
                att[lax.rem(mb - m + mps, mps), lax.rem(xb - x + spans, spans), :, cols] = result[xb, mb]

    @pl.when((s > 0) & (s < last))
    def _():
        pl.semaphore_wait(relay, 1)
        pl.semaphore_signal(relay, 1, device_id={"section": succ})

    @pl.when(s == last)
    def _():
        pl.semaphore_wait(relay, 1)

    for load in loads[2:]:
        load.wait()
    level = level_ref[0]

    def to_mp(j, c):
        return pltpu.make_async_remote_copy(
            send_mp.at[j - 1, c], recv_mp.at[j - 1, c], mp_send.at[j - 1, c], mp_recv.at[j - 1, c],
            device_id={"mp": lax.rem(m + j, mps)},
        )

    def to_span(i, c):
        return pltpu.make_async_remote_copy(
            send_span.at[i - 1, c], recv_span.at[i - 1, c],
            span_send.at[i - 1, c], span_recv.at[i - 1, c],
            device_id={"span": lax.rem(x + i, spans)},
        )

    def to_next(c):
        return pltpu.make_async_remote_copy(
            send_next.at[c], out_hbm.at[0, :, chunk_cols(c)], next_send.at[c], next_recv.at[c],
            device_id={"section": succ},
        )

    def project(c):
        part = jnp.dot(
            att[...].reshape(tokens, width), w_buf[:, chunk_cols(c)],
            preferred_element_type=jnp.float32,
        ).reshape(mps, spans, rows, chunk)
        for j in range(1, mps):
            send_mp[j - 1, c] = part[j].astype(jnp.bfloat16)
            to_mp(j, c).start()
        keep[c] = part[0]

    def reduce_mp(c):
        total = keep[c]
        for j in range(1, mps):
            to_mp(j, c).wait_recv()
            total = total + recv_mp[j - 1, c].astype(jnp.float32)
        for i in range(1, spans):
            send_span[i - 1, c] = total[i].astype(jnp.bfloat16)
            to_span(i, c).start()
        keep[c, 0] = total[0]

    def finish(c):
        total = keep[c, 0]
        for i in range(1, spans):
            to_span(i, c).wait_recv()
            total = total + recv_span[i - 1, c].astype(jnp.float32)
        table = gate_buf[:, chunk_cols(c)]
        level_ids = lax.broadcasted_iota(jnp.int32, table.shape, 0)
        gate = jnp.sum(jnp.where(level_ids == level, table, 0.0), axis=0, keepdims=True)
        updated = lat_buf[:, chunk_cols(c)].astype(jnp.float32) + gate * total
        send_next[c] = updated.astype(jnp.bfloat16)
        to_next(c).start()

    @pl.loop(0, chunks + lag_span)
    def _(step):
        @pl.when(step < chunks)
        def _():
            project(step)

        @pl.when((step >= lag_mp) & (step < chunks + lag_mp))
        def _():
            reduce_mp(step - lag_mp)

        @pl.when(step >= lag_span)
        def _():
            finish(step - lag_span)

    @pl.loop(0, heads)
    def _(h):
        @pl.when(s < last)
        def _():
            up(h).wait_send()

        @pl.when(s > 0)
        def _():
            down(h).wait_send()

    @pl.loop(0, chunks)
    def _(c):
        for j in range(1, mps):
            to_mp(j, c).wait_send()
        for i in range(1, spans):
            to_span(i, c).wait_send()
        to_next(c).wait()


def shards(sizes, queries, keys_values, latents, out_weight, gate_table, level_index, pair_window):
    sections, spans, mps = sizes
    tokens, width = queries.shape[1:]
    rows, model = latents.shape[1:]
    heads = width // HD
    chunk = CHUNK if model % CHUNK == 0 else HD
    chunks = model // chunk
    bf16, f32 = jnp.bfloat16, jnp.float32
    dma = pltpu.SemaphoreType.DMA
    hbm = pl.BlockSpec(memory_space=pltpu.HBM)
    return pl.pallas_call(
        functools.partial(fused, sections, spans, mps, chunk, LAG_MP, LAG_SPAN),
        out_shape=jax.ShapeDtypeStruct(latents.shape, bf16),
        in_specs=[hbm, hbm, hbm, hbm, hbm, hbm, hbm],
        out_specs=hbm,
        scratch_shapes=[
            pltpu.VMEM((tokens, width), bf16),
            pltpu.VMEM((2, tokens, width), bf16),
            pltpu.VMEM((rows, model), bf16),
            pltpu.VMEM(out_weight.shape, bf16),
            pltpu.VMEM(gate_table.shape, f32),
            pltpu.VMEM((heads, 2, tokens, HD), bf16),
            pltpu.VMEM((heads, 2, tokens, HD), bf16),
            pltpu.VMEM((mps, spans, rows, width), bf16),
            pltpu.VMEM((chunks, spans, rows, chunk), f32),
            pltpu.VMEM((mps - 1, chunks, spans, rows, chunk), bf16),
            pltpu.VMEM((mps - 1, chunks, spans, rows, chunk), bf16),
            pltpu.VMEM((spans - 1, chunks, rows, chunk), bf16),
            pltpu.VMEM((spans - 1, chunks, rows, chunk), bf16),
            pltpu.VMEM((chunks, rows, chunk), bf16),
            pltpu.SMEM(level_index.shape, jnp.int32),
            pltpu.SMEM(pair_window.shape, jnp.int32),
            dma((7,)),
            dma((heads,)), dma((heads,)), dma((heads,)), dma((heads,)),
            dma((mps - 1, chunks)), dma((mps - 1, chunks)),
            dma((spans - 1, chunks)), dma((spans - 1, chunks)),
            dma((chunks,)), dma((chunks,)),
            pltpu.SemaphoreType.REGULAR,
        ],
        compiler_params=pltpu.CompilerParams(
            collective_id=0, has_side_effects=True, vmem_limit_bytes=60 * 1024 * 1024
        ),
    )(level_index, pair_window, queries, keys_values, latents, out_weight, gate_table)


def solution(mesh):
    sizes = (mesh.shape["section"], mesh.shape["span"], mesh.shape["mp"])
    in_specs = (
        P(("group", "section"), None, ("span", "mp")),
        P(None, ("group", "section"), None, ("span", "mp")),
        P(("group", "section"), ("span", "mp"), None),
        P(("span", "mp"), None),
        P(),
        P(("group", "section")),
        P("group"),
    )
    out_specs = P(("group", "section"), ("span", "mp"), None)
    return jax.shard_map(
        functools.partial(shards, sizes), mesh=mesh, in_specs=in_specs, out_specs=out_specs,
        check_vma=False,
    )
```

```python
import functools
import math

import jax
import jax.numpy as jnp
from jax import lax
from jax.experimental import pallas as pl
from jax.experimental.pallas import tpu as pltpu
from jax.sharding import PartitionSpec as P

HD = 128
NEG_BIG = -1e30
CHUNK = 256
LAG_MP = 3
LAG_SPAN = 8


def fused(
    sections, spans, mps, chunk, lag_mp, lag_span,
    level_hbm, window_hbm, q_hbm, kv_hbm, lat_hbm, w_hbm, gate_hbm, out_hbm,
    q_buf, kv_buf, lat_buf, w_buf, gate_buf, below, above, att, keep,
    send_mp, recv_mp, send_span, recv_span, send_next,
    level_ref, window_ref, load_sems, up_send, up_recv, down_send, down_recv,
    mp_send, mp_recv, span_send, span_recv, next_send, next_recv, relay,
):
    s = lax.axis_index("section")
    x = lax.axis_index("span")
    m = lax.axis_index("mp")
    last = sections - 1
    heads = below.shape[0]
    tokens = kv_buf.shape[1]
    width = kv_buf.shape[2]
    rows = lat_buf.shape[0]
    chunks = keep.shape[0]
    succ = lax.rem(s + 1, sections)
    pred = lax.rem(s + sections - 1, sections)

    barrier = pltpu.get_barrier_semaphore()

    @pl.when(s < last)
    def _():
        pl.semaphore_signal(barrier, 1, device_id={"section": succ})

    @pl.when(s > 0)
    def _():
        pl.semaphore_signal(barrier, 1, device_id={"section": pred})

    for j in range(1, mps):
        pl.semaphore_signal(barrier, 1, device_id={"mp": lax.rem(m + j, mps)})
    for i in range(1, spans):
        pl.semaphore_signal(barrier, 1, device_id={"span": lax.rem(x + i, spans)})
    others = mps - 1 + spans - 1

    windows = pltpu.make_async_copy(window_hbm, window_ref, load_sems.at[6])
    loads = [
        pltpu.make_async_copy(q_hbm.at[0], q_buf, load_sems.at[0]),
        pltpu.make_async_copy(kv_hbm.at[:, 0], kv_buf, load_sems.at[1]),
        pltpu.make_async_copy(lat_hbm.at[0], lat_buf, load_sems.at[2]),
        pltpu.make_async_copy(gate_hbm, gate_buf, load_sems.at[3]),
        pltpu.make_async_copy(w_hbm, w_buf, load_sems.at[4]),
        pltpu.make_async_copy(level_hbm, level_ref, load_sems.at[5]),
    ]

    @pl.when((s > 0) & (s < last))
    def _():
        pl.semaphore_wait(barrier, others + 2)

    @pl.when((s == 0) | (s == last))
    def _():
        pl.semaphore_wait(barrier, others + 1)

    def head_cols(h):
        return pl.ds(pl.multiple_of(h * HD, HD), HD)

    def chunk_cols(c):
        return pl.ds(pl.multiple_of(c * chunk, chunk), chunk)

    def up(h):
        return pltpu.make_async_remote_copy(
            kv_hbm.at[:, 0, :, head_cols(h)], below.at[h], up_send.at[h], up_recv.at[h],
            device_id={"section": succ},
        )

    def down(h):
        return pltpu.make_async_remote_copy(
            kv_hbm.at[:, 0, :, head_cols(h)], above.at[h], down_send.at[h], down_recv.at[h],
            device_id={"section": pred},
        )

    @pl.loop(0, heads)
    def _(h):
        @pl.when(s < last)
        def _():
            up(h).start()

    @pl.loop(0, heads)
    def _(h):
        @pl.when(s > 0)
        def _():
            down(h).start()

    windows.start()
    for load in loads:
        load.start()

    @pl.when(s == 0)
    def _():
        below[...] = jnp.zeros_like(below)
        pl.semaphore_signal(relay, 1, device_id={"section": succ})

    @pl.when(s == last)
    def _():
        above[...] = jnp.zeros_like(above)

    windows.wait()
    pairs = window_ref.shape[0]
    w_lo = jnp.where(s > 0, window_ref[jnp.clip(s - 1, 0, pairs - 1)], 0)
    w_hi = jnp.where(s < last, window_ref[jnp.clip(s, 0, pairs - 1)], 0)
    key_ids = lax.broadcasted_iota(jnp.int32, (1, tokens), 1)
    mask_lo = key_ids >= tokens - w_lo
    mask_hi = key_ids < w_hi
    scale = 1.0 / math.sqrt(HD)
    loads[0].wait()
    loads[1].wait()

    def score(q, k):
        return lax.dot_general(
            q, k, (((1,), (1,)), ((), ())), preferred_element_type=jnp.float32
        ) * scale

    @pl.loop(0, heads)
    def _(h):
        cols = head_cols(h)
        q = q_buf[:, cols]
        s_own = score(q, kv_buf[0, :, cols])

        @pl.when(s > 0)
        def _():
            up(h).wait_recv()

        @pl.when(s < last)
        def _():
            down(h).wait_recv()

        s_lo = jnp.where(mask_lo, score(q, below[h, 0]), NEG_BIG)
        s_hi = jnp.where(mask_hi, score(q, above[h, 0]), NEG_BIG)
        top = jnp.max(jnp.maximum(jnp.maximum(s_lo, s_hi), s_own), axis=1, keepdims=True)
        p_lo = jnp.exp(s_lo - top)
        p_own = jnp.exp(s_own - top)
        p_hi = jnp.exp(s_hi - top)
        total = jnp.sum(p_lo + p_own + p_hi, axis=1, keepdims=True)
        weighted = (
            jnp.dot(p_own.astype(jnp.bfloat16), kv_buf[1, :, cols], preferred_element_type=jnp.float32)
            + jnp.dot(p_lo.astype(jnp.bfloat16), below[h, 1], preferred_element_type=jnp.float32)
            + jnp.dot(p_hi.astype(jnp.bfloat16), above[h, 1], preferred_element_type=jnp.float32)
        )
        result = (weighted / total).astype(jnp.bfloat16).reshape(spans, mps, rows, HD)
        for xb in range(spans):
            for mb in range(mps):
                att[lax.rem(mb - m + mps, mps), lax.rem(xb - x + spans, spans), :, cols] = result[xb, mb]

    @pl.when((s > 0) & (s < last))
    def _():
        pl.semaphore_wait(relay, 1)
        pl.semaphore_signal(relay, 1, device_id={"section": succ})

    @pl.when(s == last)
    def _():
        pl.semaphore_wait(relay, 1)

    for load in loads[2:]:
        load.wait()
    level = level_ref[0]

    def to_mp(j, c):
        return pltpu.make_async_remote_copy(
            send_mp.at[j - 1, c], recv_mp.at[j - 1, c], mp_send.at[j - 1, c], mp_recv.at[j - 1, c],
            device_id={"mp": lax.rem(m + j, mps)},
        )

    def to_span(i, c):
        return pltpu.make_async_remote_copy(
            send_span.at[i - 1, c], recv_span.at[i - 1, c],
            span_send.at[i - 1, c], span_recv.at[i - 1, c],
            device_id={"span": lax.rem(x + i, spans)},
        )

    def to_next(c):
        return pltpu.make_async_remote_copy(
            send_next.at[c], out_hbm.at[0, :, chunk_cols(c)], next_send.at[c], next_recv.at[c],
            device_id={"section": succ},
        )

    def project(c):
        part = jnp.dot(
            att[...].reshape(tokens, width), w_buf[:, chunk_cols(c)],
            preferred_element_type=jnp.float32,
        ).reshape(mps, spans, rows, chunk)
        for j in range(1, mps):
            send_mp[j - 1, c] = part[j].astype(jnp.bfloat16)
            to_mp(j, c).start()
        keep[c] = part[0]

    def reduce_mp(c):
        total = keep[c]
        for j in range(1, mps):
            to_mp(j, c).wait_recv()
            total = total + recv_mp[j - 1, c].astype(jnp.float32)
        for i in range(1, spans):
            send_span[i - 1, c] = total[i].astype(jnp.bfloat16)
            to_span(i, c).start()
        keep[c, 0] = total[0]

    def finish(c):
        total = keep[c, 0]
        for i in range(1, spans):
            to_span(i, c).wait_recv()
            total = total + recv_span[i - 1, c].astype(jnp.float32)
        table = gate_buf[:, chunk_cols(c)]
        level_ids = lax.broadcasted_iota(jnp.int32, table.shape, 0)
        gate = jnp.sum(jnp.where(level_ids == level, table, 0.0), axis=0, keepdims=True)
        updated = lat_buf[:, chunk_cols(c)].astype(jnp.float32) + gate * total
        send_next[c] = updated.astype(jnp.bfloat16)
        to_next(c).start()

    @pl.loop(0, chunks + lag_span)
    def _(step):
        @pl.when(step < chunks)
        def _():
            project(step)

        @pl.when((step >= lag_mp) & (step < chunks + lag_mp))
        def _():
            reduce_mp(step - lag_mp)

        @pl.when(step >= lag_span)
        def _():
            finish(step - lag_span)

    @pl.loop(0, heads)
    def _(h):
        @pl.when(s < last)
        def _():
            up(h).wait_send()

        @pl.when(s > 0)
        def _():
            down(h).wait_send()

    @pl.loop(0, chunks)
    def _(c):
        for j in range(1, mps):
            to_mp(j, c).wait_send()
        for i in range(1, spans):
            to_span(i, c).wait_send()
        to_next(c).wait()


def shards(sizes, queries, keys_values, latents, out_weight, gate_table, level_index, pair_window):
    sections, spans, mps = sizes
    tokens, width = queries.shape[1:]
    rows, model = latents.shape[1:]
    heads = width // HD
    chunk = CHUNK if model % CHUNK == 0 else HD
    chunks = model // chunk
    bf16, f32 = jnp.bfloat16, jnp.float32
    dma = pltpu.SemaphoreType.DMA
    hbm = pl.BlockSpec(memory_space=pltpu.HBM)
    return pl.pallas_call(
        functools.partial(fused, sections, spans, mps, chunk, LAG_MP, LAG_SPAN),
        out_shape=jax.ShapeDtypeStruct(latents.shape, bf16),
        in_specs=[hbm, hbm, hbm, hbm, hbm, hbm, hbm],
        out_specs=hbm,
        scratch_shapes=[
            pltpu.VMEM((tokens, width), bf16),
            pltpu.VMEM((2, tokens, width), bf16),
            pltpu.VMEM((rows, model), bf16),
            pltpu.VMEM(out_weight.shape, bf16),
            pltpu.VMEM(gate_table.shape, f32),
            pltpu.VMEM((heads, 2, tokens, HD), bf16),
            pltpu.VMEM((heads, 2, tokens, HD), bf16),
            pltpu.VMEM((mps, spans, rows, width), bf16),
            pltpu.VMEM((chunks, spans, rows, chunk), f32),
            pltpu.VMEM((mps - 1, chunks, spans, rows, chunk), bf16),
            pltpu.VMEM((mps - 1, chunks, spans, rows, chunk), bf16),
            pltpu.VMEM((spans - 1, chunks, rows, chunk), bf16),
            pltpu.VMEM((spans - 1, chunks, rows, chunk), bf16),
            pltpu.VMEM((chunks, rows, chunk), bf16),
            pltpu.SMEM(level_index.shape, jnp.int32),
            pltpu.SMEM(pair_window.shape, jnp.int32),
            dma((7,)),
            dma((heads,)), dma((heads,)), dma((heads,)), dma((heads,)),
            dma((mps - 1, chunks)), dma((mps - 1, chunks)),
            dma((spans - 1, chunks)), dma((spans - 1, chunks)),
            dma((chunks,)), dma((chunks,)),
            pltpu.SemaphoreType.REGULAR,
        ],
        compiler_params=pltpu.CompilerParams(
            collective_id=0, has_side_effects=True, vmem_limit_bytes=60 * 1024 * 1024
        ),
    )(level_index, pair_window, queries, keys_values, latents, out_weight, gate_table)


def solution(mesh):
    sizes = (mesh.shape["section"], mesh.shape["span"], mesh.shape["mp"])
    in_specs = (
        P(("group", "section"), None, ("span", "mp")),
        P(None, ("group", "section"), None, ("span", "mp")),
        P(("group", "section"), ("span", "mp"), None),
        P(("span", "mp"), None),
        P(),
        P(("group", "section")),
        P("group"),
    )
    out_specs = P(("group", "section"), ("span", "mp"), None)
    return jax.shard_map(
        functools.partial(shards, sizes), mesh=mesh, in_specs=in_specs, out_specs=out_specs,
        check_vma=False,
    )
```
